32 devices in a mesh: ctx: 8 (over z, x), mp: 4 (over y, core).
Axes of the slice: x: 2, y: 2, z: 4, core: 2. Of those that a mesh axis runs over, the one named last changes fastest.
Arguments:
- tokens: bfloat16 [1024, 2048], P('ctx'), may hold values from -6 to 6
- out_grad: bfloat16 [1024, 2048], P('ctx'), may hold values from -6 to 6
- attn_gain: bfloat16 [2048], P('ctx'), may hold values from 0.5 to 1.5
- query_weight: bfloat16 [2048, 2048], P('ctx', 'mp'), may hold values from -0.125 to 0.125
- key_weight: bfloat16 [2048, 2048], P('ctx', 'mp'), may hold values from -0.125 to 0.125
- value_weight: bfloat16 [2048, 2048], P('ctx', 'mp'), may hold values from -0.125 to 0.125
- query_gain: bfloat16 [2048], P(('mp', 'ctx')), may hold values from 0.25 to 1.75
- key_gain: bfloat16 [2048], P(('mp', 'ctx')), may hold values from 0.5 to 1.5
- output_weight: bfloat16 [2048, 2048], P('mp', 'ctx'), may hold values from -0.375 to 0.375
- ffn_gain: bfloat16 [2048], P('ctx'), may hold values from 0.5 to 1.5
- router_weight: bfloat16 [2048, 64], P('ctx'), may hold values from -0.25 to 0.25
- gate_experts: bfloat16 [64, 2048, 1024], P('ctx', None, 'mp'), may hold values from -0.125 to 0.125
- up_experts: bfloat16 [64, 2048, 1024], P('ctx', None, 'mp'), may hold values from -0.125 to 0.125
- down_experts: bfloat16 [64, 1024, 2048], P('ctx', 'mp'), may hold values from -3 to 3
- expert_ids: int32 [1024, 8], P('ctx'), may hold values from 0 to 63, all different within a row; in each aligned block of 128 rows (0 to 127, 128 to 255, ...) at most 20 rows name the same one
- block_order: int32 [16], replicated, may hold values from 0 to 15, each once
Outputs:
- block_out: bfloat16 [1024, 2048], P('ctx')
- tokens_grad: float32 [1024, 2048], P('ctx')
- attn_gain_grad: float32 [2048], P('ctx')
- query_weight_grad: float32 [2048, 2048], P('ctx', 'mp')
- key_weight_grad: float32 [2048, 2048], P('ctx', 'mp')
- value_weight_grad: float32 [2048, 2048], P('ctx', 'mp')
- query_gain_grad: float32 [2048], P(('mp', 'ctx'))
- key_gain_grad: float32 [2048], P(('mp', 'ctx'))
- output_weight_grad: float32 [2048, 2048], P('mp', 'ctx')
- ffn_gain_grad: float32 [2048], P('ctx')
- router_weight_grad: float32 [2048, 64], P('ctx')
- gate_experts_grad: float32 [64, 2048, 1024], P('ctx', None, 'mp')
- up_experts_grad: float32 [64, 2048, 1024], P('ctx', None, 'mp')
- down_experts_grad: float32 [64, 1024, 2048], P('ctx', 'mp')
The draws below stay inside these ranges and needn't reach their ends.
Inputs may be any that keep to these rules, and one draw needn't show every extreme that they name: `expert_ids`: each row names 8 different experts. The 128 rows of one device name no expert more than 20 times, and in every draw some device names some expert exactly 20 times. A permutation of the blocks: storage block j holds the positions block_order[j] * 64 to block_order[j] * 64 + 63.
All inputs are finite; a program needn't handle non-finite values.
Results may differ from the reference program's by a relative error of at most 0.03.
Values may be sent and summed in bfloat16 or wider, within the bound.
No kernel may reach another device: no remote copies, remote signals or barrier semaphores. Data moves between devices by JAX's collectives and lax.ppermute only.
A program may use at most 256 MiB of HBM per device.

```python
import math
import jax
import jax.numpy as jnp
import numpy as np
from jax import lax

D = 2048
HEADS = 16
HEAD_DIM = 128
FF = 1024
EXPERTS = 64
TOPK = 8
TOK_DEV = 128
TOKENS = 1024
BLK = 64
NBLK = 16
CAP = 20
N_CTX = 8
N_MP = 4


def shard_levels(rng, shape, cuts, low, largest):
    def one(axis_at, blocks):
        draws = jax.random.uniform(jax.random.fold_in(jax.random.fold_in(rng, 6), axis_at), (blocks,), jnp.float32, low / len(cuts), largest / len(cuts))
        return jnp.repeat(jnp.exp(draws), shape[axis_at] // blocks).reshape((-1,) + (1,) * (len(shape) - axis_at - 1))

    loudness = one(*cuts[0])
    for cut in cuts[1:]:
        loudness = loudness * one(*cut)
    return loudness


def deal_out(key, own, number, rows, amount, top, most, lean):
    sequence = jax.random.permutation(key, amount)
    packed, common = shares(amount, rows * top, most, lean, True), shares(amount, rows * top, most, lean, False)
    places = jnp.arange(amount)

    def named(tallies, turn):
        used = int((tallies > 0).sum())
        fixed = max(1, used // 4)
        shifted = fixed + (places - fixed + turn * (used - fixed)) % max(1, amount - fixed)
        return jnp.zeros((amount,), jnp.int32).at[sequence[jnp.where(places < fixed, places, shifted)]].set(jnp.asarray(tallies, jnp.int32))

    tallies = jnp.where(number % 4 == 0, named(packed, number // 4), named(common, number - number // 4 - 1))
    mixed = jax.random.permutation(jax.random.fold_in(own, 3), amount)
    source_of, receiver = mixed[0:amount // 2 * 2:2], mixed[1:amount // 2 * 2:2]
    margin = jnp.minimum(tallies[source_of] - 1, most - tallies[receiver]) // 2
    margin = jnp.where((source_of == sequence[0]) | (receiver == sequence[0]) | (tallies[receiver] == 0), 0, jnp.maximum(margin, 0))
    shifted = jax.random.randint(jax.random.fold_in(own, 4), (amount // 2,), 0, 1 << 20) % (margin + 1)
    tallies = tallies.at[source_of].add(-shifted).at[receiver].add(shifted)
    items = jnp.searchsorted(jnp.cumsum(tallies), jnp.arange(rows * top), side="right").astype(jnp.int32)
    listing = items.reshape(top, rows).T
    listing = listing[jax.random.permutation(jax.random.fold_in(own, 1), rows)]
    turn = jax.random.randint(jax.random.fold_in(own, 2), (rows, 1), 0, top)
    return jnp.take_along_axis(listing, (jnp.arange(top)[None, :] + turn) % top, axis=1)


def shares(amount, total, bound, skew, full):
    loads = [(1 << 20) // math.isqrt(standing ** skew) + 1 for standing in range(1, amount + 1)]
    largest = bound if full else min(bound, max(-(-total // amount), total * loads[0] // sum(loads)))
    least = 1 if total - largest >= amount - 1 else 0
    counts, spare = [largest] + [least] * (amount - 1), total - largest - least * (amount - 1)
    while spare > 0:
        candidates = [i for i in range(1, amount) if counts[i] < largest] or [i for i in range(1, amount) if counts[i] < bound]
        whole, budget = sum([loads[i] for i in candidates]), spare
        for i in candidates:
            more = min(bound - counts[i], max(1, budget * loads[i] // whole), spare)
            counts[i] = counts[i] + more
            spare = spare - more
    return np.array(counts)


def gaussian(stream_key, shape, width, bound, shards=(), held_as=jnp.bfloat16):
    factor_of = shard_levels(stream_key, shape, shards, -0.22, 0.18) if shards else 1.0
    array = jax.random.normal(stream_key, shape, jnp.float32) * width * factor_of
    return jnp.minimum(jnp.maximum(array, -bound), bound).astype(held_as)


def setup_inputs(seed: int = 0) -> dict:
    key_of = jax.random.split(jax.random.key(seed), 17)
    tokens = gaussian(key_of[0], (TOKENS, D), 1.0, 6.0, ((0, 8),))
    out_grad = gaussian(key_of[1], (TOKENS, D), 1.0, 6.0, ((0, 8),))
    attn_gain = jnp.clip(1.0 + 0.1 * jax.random.normal(key_of[2], (D,), jnp.float32), 0.5, 1.5).astype(jnp.bfloat16)
    query_weight = gaussian(key_of[3], (D, D), D ** -0.5, 0.125, ((0, 8), (1, 4)))
    key_weight = gaussian(key_of[4], (D, D), D ** -0.5, 0.125, ((0, 8), (1, 4)))
    value_weight = gaussian(key_of[5], (D, D), D ** -0.5, 0.125, ((0, 8), (1, 4)))
    query_gain = jnp.clip(1.0 + 0.15 * jax.random.normal(key_of[6], (D,), jnp.float32), 0.25, 1.75).astype(jnp.bfloat16)
    key_gain = jnp.clip(1.0 + 0.1 * jax.random.normal(key_of[7], (D,), jnp.float32), 0.5, 1.5).astype(jnp.bfloat16)
    output_weight = gaussian(key_of[8], (D, D), (D // 8) ** -0.5, 0.375, ((0, 4), (1, 8)))
    ffn_gain = jnp.clip(1.0 + 0.1 * jax.random.normal(key_of[9], (D,), jnp.float32), 0.5, 1.5).astype(jnp.bfloat16)
    router_weight = gaussian(key_of[10], (D, EXPERTS), (D // 4) ** -0.5, 0.25, ((0, 8),))
    gate_experts = gaussian(key_of[11], (EXPERTS, D, FF), D ** -0.5, 0.125, ((0, 8), (2, 4)))
    up_experts = gaussian(key_of[12], (EXPERTS, D, FF), D ** -0.5, 0.125, ((0, 8), (2, 4)))
    down_experts = gaussian(key_of[13], (EXPERTS, FF, D), (max(FF // 256, 1)) ** -0.5, 3.0, ((0, 8), (1, 4)))
    expert_ids_keys = jax.random.split(jax.random.fold_in(key_of[14], 1), TOKENS // TOK_DEV)
    expert_ids_turns = jax.random.permutation(jax.random.fold_in(key_of[14], 3), TOKENS // TOK_DEV)
    expert_ids = jax.vmap(lambda own, number: deal_out(jax.random.fold_in(key_of[14], 2), own, number, TOK_DEV, EXPERTS, TOPK, CAP, 2))(expert_ids_keys, expert_ids_turns).reshape((TOKENS, TOPK))
    block_order = jax.random.permutation(key_of[15], NBLK).astype(jnp.int32)
    return dict(tokens=tokens, out_grad=out_grad, attn_gain=attn_gain, query_weight=query_weight, key_weight=key_weight, value_weight=value_weight, query_gain=query_gain, key_gain=key_gain, output_weight=output_weight, ffn_gain=ffn_gain, router_weight=router_weight, gate_experts=gate_experts, up_experts=up_experts, down_experts=down_experts, expert_ids=expert_ids, block_order=block_order)


EPSILON = 1e-05
ROPE_BASE = 10000.0
HIGHEST = lax.Precision.HIGHEST

def rms_scale(values):
    return lax.rsqrt(lax.optimization_barrier(jnp.mean(values * values, axis=-1)) + EPSILON)

def round_low(values):
    return lax.optimization_barrier(values.astype(jnp.bfloat16)).astype(jnp.float32)

def rope_tables(positions):
    half_dim = HEAD_DIM // 2
    frequency = ROPE_BASE ** (-(jnp.arange(half_dim, dtype=jnp.float32) * (2.0 / HEAD_DIM)))
    angles = positions.astype(jnp.float32)[:, None] * frequency[None, :]
    cosine_table = jnp.cos(angles)
    sine_table = jnp.sin(angles)
    return (jnp.concatenate([cosine_table, cosine_table], 1), jnp.concatenate([sine_table, sine_table], 1))

def rotate(values, cosine_table, sine_table):
    half_dim = values.shape[-1] // 2
    turned = jnp.concatenate([-values[..., half_dim:], values[..., :half_dim]], -1)
    return values * cosine_table[:, None, :] + turned * sine_table[:, None, :]

def unrotate(gradient, cosine_table, sine_table):
    half_dim = gradient.shape[-1] // 2
    scaled = gradient * sine_table[:, None, :]
    turned = jnp.concatenate([scaled[..., half_dim:], -scaled[..., :half_dim]], -1)
    return gradient * cosine_table[:, None, :] + turned

def expert_pass(rows_in, grads_in, gate_weight, up_weight, down_weight):
    act_gate = jnp.dot(rows_in, gate_weight, preferred_element_type=jnp.float32)
    act_up = jnp.dot(rows_in, up_weight, preferred_element_type=jnp.float32)
    sigmoid_gate = jax.nn.sigmoid(act_gate)
    swish_gate = act_gate * sigmoid_gate
    inner_act = (swish_gate * act_up).astype(jnp.bfloat16)
    inner_grad = jnp.dot(grads_in, down_weight.T, preferred_element_type=jnp.float32)
    gate_pre = (inner_grad * act_up * sigmoid_gate * (1.0 + act_gate * (1.0 - sigmoid_gate))).astype(jnp.bfloat16)
    up_pre = (inner_grad * swish_gate).astype(jnp.bfloat16)
    quarter = FF // N_MP
    out_total = jnp.zeros((rows_in.shape[0], D), jnp.float32)
    back_total = jnp.zeros((rows_in.shape[0], D), jnp.float32)
    for part_index in range(N_MP):
        low_col = part_index * quarter
        high_col = low_col + quarter
        out_piece = jnp.dot(inner_act[:, low_col:high_col], down_weight[low_col:high_col], preferred_element_type=jnp.float32)
        out_total = out_total + round_low(out_piece)
        back_piece = jnp.dot(gate_pre[:, low_col:high_col], gate_weight[:, low_col:high_col].T, preferred_element_type=jnp.float32)
        back_piece = back_piece + jnp.dot(up_pre[:, low_col:high_col], up_weight[:, low_col:high_col].T, preferred_element_type=jnp.float32)
        back_total = back_total + round_low(back_piece)
    down_grad = jnp.dot(inner_act.T, grads_in, preferred_element_type=jnp.float32)
    gate_grad = jnp.dot(rows_in.T, gate_pre, preferred_element_type=jnp.float32)
    up_grad = jnp.dot(rows_in.T, up_pre, preferred_element_type=jnp.float32)
    return (out_total, back_total, gate_grad, up_grad, down_grad)

def reference(tokens, out_grad, attn_gain, query_weight, key_weight, value_weight, query_gain, key_gain, output_weight, ffn_gain, router_weight, gate_experts, up_experts, down_experts, expert_ids, block_order):
    row_block = math.gcd(512, TOKENS)
    score_scale = 1.0 / math.sqrt(HEAD_DIM)
    hidden_in = tokens.astype(jnp.float32)
    grad_rows = out_grad.astype(jnp.float32)
    gain_one = attn_gain.astype(jnp.float32)
    gain_two = ffn_gain.astype(jnp.float32)
    gain_query = query_gain.astype(jnp.float32)
    gain_key = key_gain.astype(jnp.float32)
    scale_one = rms_scale(hidden_in)
    normed_one = (hidden_in * scale_one[:, None] * gain_one).astype(jnp.bfloat16)
    query_raw = jnp.dot(normed_one, query_weight, preferred_element_type=jnp.float32)
    key_raw = jnp.dot(normed_one, key_weight, preferred_element_type=jnp.float32)
    value_rows = jnp.dot(normed_one, value_weight, preferred_element_type=jnp.float32).astype(jnp.bfloat16)
    query_scale = rms_scale(query_raw)
    key_scale = rms_scale(key_raw)
    positions = (block_order[:, None] * BLK + jnp.arange(BLK, dtype=jnp.int32)[None, :]).reshape(TOKENS)
    cosine_table, sine_table = rope_tables(positions)
    query_rot = rotate((query_raw * query_scale[:, None] * gain_query).reshape(TOKENS, HEADS, HEAD_DIM), cosine_table, sine_table).astype(jnp.bfloat16)
    key_rot = rotate((key_raw * key_scale[:, None] * gain_key).reshape(TOKENS, HEADS, HEAD_DIM), cosine_table, sine_table).astype(jnp.bfloat16)
    key_wide = key_rot.astype(jnp.float32)
    value_wide = value_rows.reshape(TOKENS, HEADS, HEAD_DIM).astype(jnp.float32)
    starts = jnp.arange(0, TOKENS, row_block, dtype=jnp.int32)

    def forward_block(first_row):
        query_block = lax.dynamic_slice_in_dim(query_rot, first_row, row_block, 0).astype(jnp.float32)
        query_pos = lax.dynamic_slice_in_dim(positions, first_row, row_block, 0)
        allowed = (positions[None, :] <= query_pos[:, None])[:, None, :]
        scores = jnp.einsum('rhd,khd->rhk', query_block, key_wide, precision=HIGHEST) * score_scale
        row_max = lax.optimization_barrier(jnp.max(jnp.where(allowed, scores, -jnp.inf), axis=-1))
        weights = jnp.where(allowed, jnp.exp(scores - row_max[..., None]), 0.0)
        row_total = lax.optimization_barrier(jnp.sum(weights, axis=-1))
        heads_block = jnp.einsum('rhk,khd->rhd', weights, value_wide, precision=HIGHEST) / row_total[..., None]
        return (heads_block.astype(jnp.bfloat16), row_max + jnp.log(row_total))
    heads_blocks, lse_blocks = lax.map(forward_block, starts)
    heads_out = heads_blocks.reshape(TOKENS, D)
    log_total = lse_blocks.reshape(TOKENS, HEADS)
    residual = hidden_in + jnp.dot(heads_out, output_weight, preferred_element_type=jnp.float32)
    scale_two = rms_scale(residual)
    normed_two = (residual * scale_two[:, None] * gain_two).astype(jnp.bfloat16)
    router_probs = jax.nn.softmax(jnp.dot(normed_two, router_weight, preferred_element_type=jnp.float32), axis=-1)
    gate_values = jnp.take_along_axis(router_probs, expert_ids, axis=1)
    pair_ids = expert_ids.reshape(TOKENS * TOPK)
    pick_table = (pair_ids[:, None] == jnp.arange(EXPERTS, dtype=jnp.int32)[None, :]).astype(jnp.int32)
    running = jnp.cumsum(pick_table.reshape(N_CTX, TOK_DEV * TOPK, EXPERTS), axis=1).reshape(TOKENS * TOPK, EXPERTS)
    slot_pos = lax.optimization_barrier(jnp.sum(pick_table * (running - 1), axis=1))
    device_of = jnp.arange(TOKENS * TOPK, dtype=jnp.int32) // (TOK_DEV * TOPK)
    per_expert = N_CTX * CAP
    slot_index = pair_ids * per_expert + device_of * CAP + slot_pos
    sent_grads = (gate_values[:, :, None] * grad_rows[:, None, :]).astype(jnp.bfloat16).reshape(TOKENS * TOPK, D)
    expert_rows = jnp.zeros((EXPERTS * per_expert, D), jnp.bfloat16).at[slot_index].set(jnp.repeat(normed_two, TOPK, axis=0)).reshape(EXPERTS, per_expert, D)
    expert_grads = jnp.zeros((EXPERTS * per_expert, D), jnp.bfloat16).at[slot_index].set(sent_grads).reshape(EXPERTS, per_expert, D)

    def expert_step(unused, inputs):
        return (unused, expert_pass(*inputs))
    ignored, results = lax.scan(expert_step, jnp.zeros((), jnp.float32), (expert_rows, expert_grads, gate_experts, up_experts, down_experts))
    out_all, back_all, gate_experts_grad, up_experts_grad, down_experts_grad = results
    pair_out = out_all.reshape(EXPERTS * per_expert, D)[slot_index].reshape(TOKENS, TOPK, D)
    pair_back = back_all.reshape(EXPERTS * per_expert, D)[slot_index].reshape(TOKENS, TOPK, D)
    moe_full = lax.optimization_barrier(jnp.sum(gate_values[:, :, None] * pair_out, axis=1))
    block_out = (residual + moe_full).astype(jnp.bfloat16)
    gate_dots = lax.optimization_barrier(jnp.sum(pair_out * grad_rows[:, None, :], axis=2))
    choose = expert_ids[:, :, None] == jnp.arange(EXPERTS, dtype=jnp.int32)[None, None, :]
    spread_dots = lax.optimization_barrier(jnp.sum(jnp.where(choose, gate_dots[:, :, None], 0.0), axis=1))
    logit_grad = (router_probs * (spread_dots - lax.optimization_barrier(jnp.sum(gate_values * gate_dots, axis=1))[:, None])).astype(jnp.bfloat16)
    router_weight_grad = jnp.dot(normed_two.T, logit_grad, preferred_element_type=jnp.float32)
    normed_two_grad = lax.optimization_barrier(jnp.sum(pair_back, axis=1)) + jnp.dot(logit_grad, router_weight.T, preferred_element_type=jnp.float32)
    gained_two = normed_two_grad * gain_two
    ffn_gain_grad = lax.optimization_barrier(jnp.sum(normed_two_grad * residual * scale_two[:, None], axis=0))
    residual_grad = grad_rows + scale_two[:, None] * gained_two - residual * (scale_two ** 3)[:, None] * lax.optimization_barrier(jnp.mean(gained_two * residual, axis=1))[:, None]
    residual_low = residual_grad.astype(jnp.bfloat16)
    output_weight_grad = jnp.dot(heads_out.T, residual_low, preferred_element_type=jnp.float32)
    heads_grad = jnp.dot(residual_low, output_weight.T, preferred_element_type=jnp.float32).astype(jnp.bfloat16)
    heads_grad_wide = heads_grad.reshape(TOKENS, HEADS, HEAD_DIM).astype(jnp.float32)
    row_delta = lax.optimization_barrier(jnp.sum(heads_grad_wide * heads_out.reshape(TOKENS, HEADS, HEAD_DIM).astype(jnp.float32), axis=-1))

    def backward_block(running_grads, first_row):
        key_acc, value_acc = running_grads
        query_block = lax.dynamic_slice_in_dim(query_rot, first_row, row_block, 0).astype(jnp.float32)
        query_pos = lax.dynamic_slice_in_dim(positions, first_row, row_block, 0)
        grad_block = lax.dynamic_slice_in_dim(heads_grad_wide, first_row, row_block, 0)
        delta_block = lax.dynamic_slice_in_dim(row_delta, first_row, row_block, 0)
        lse_block = lax.dynamic_slice_in_dim(log_total, first_row, row_block, 0)
        allowed = (positions[None, :] <= query_pos[:, None])[:, None, :]
        scores = jnp.einsum('rhd,khd->rhk', query_block, key_wide, precision=HIGHEST) * score_scale
        weights = jnp.where(allowed, jnp.exp(scores - lse_block[..., None]), 0.0)
        weight_grad = jnp.einsum('rhd,khd->rhk', grad_block, value_wide, precision=HIGHEST)
        score_grad = round_low(weights * (weight_grad - delta_block[..., None]) * score_scale)
        query_block_grad = jnp.einsum('rhk,khd->rhd', score_grad, key_wide, precision=HIGHEST)
        key_acc = key_acc + jnp.einsum('rhk,rhd->khd', score_grad, query_block, precision=HIGHEST)
        value_acc = value_acc + jnp.einsum('rhk,rhd->khd', round_low(weights), grad_block, precision=HIGHEST)
        return ((key_acc, value_acc), query_block_grad)
    zero_heads = jnp.zeros((TOKENS, HEADS, HEAD_DIM), jnp.float32)
    (key_rot_grad, value_grad), query_blocks = lax.scan(backward_block, (zero_heads, zero_heads), starts)
    query_rot_grad = query_blocks.reshape(TOKENS, HEADS, HEAD_DIM)
    query_normed_grad = unrotate(query_rot_grad, cosine_table, sine_table).reshape(TOKENS, D)
    key_normed_grad = unrotate(key_rot_grad, cosine_table, sine_table).reshape(TOKENS, D)
    value_low = value_grad.reshape(TOKENS, D).astype(jnp.bfloat16)
    query_gain_grad = lax.optimization_barrier(jnp.sum(query_normed_grad * query_raw * query_scale[:, None], axis=0))
    key_gain_grad = lax.optimization_barrier(jnp.sum(key_normed_grad * key_raw * key_scale[:, None], axis=0))
    query_weighted = query_normed_grad * gain_query
    key_weighted = key_normed_grad * gain_key
    query_coef = lax.optimization_barrier(jnp.sum(query_weighted * query_raw, axis=1)) * query_scale ** 3 / D
    key_coef = lax.optimization_barrier(jnp.sum(key_weighted * key_raw, axis=1)) * key_scale ** 3 / D
    part_main = jnp.dot((query_weighted * query_scale[:, None]).astype(jnp.bfloat16), query_weight.T, preferred_element_type=jnp.float32)
    part_main = part_main + jnp.dot((key_weighted * key_scale[:, None]).astype(jnp.bfloat16), key_weight.T, preferred_element_type=jnp.float32)
    part_main = part_main + jnp.dot(value_low, value_weight.T, preferred_element_type=jnp.float32)
    part_query = jnp.dot(query_raw.astype(jnp.bfloat16), query_weight.T, preferred_element_type=jnp.float32)
    part_key = jnp.dot(key_raw.astype(jnp.bfloat16), key_weight.T, preferred_element_type=jnp.float32)
    normed_one_grad = part_main - query_coef[:, None] * part_query - key_coef[:, None] * part_key
    query_raw_grad = (query_weighted * query_scale[:, None] - query_raw * query_coef[:, None]).astype(jnp.bfloat16)
    key_raw_grad = (key_weighted * key_scale[:, None] - key_raw * key_coef[:, None]).astype(jnp.bfloat16)
    query_weight_grad = jnp.dot(normed_one.T, query_raw_grad, preferred_element_type=jnp.float32)
    key_weight_grad = jnp.dot(normed_one.T, key_raw_grad, preferred_element_type=jnp.float32)
    value_weight_grad = jnp.dot(normed_one.T, value_low, preferred_element_type=jnp.float32)
    gained_one = normed_one_grad * gain_one
    attn_gain_grad = lax.optimization_barrier(jnp.sum(normed_one_grad * hidden_in * scale_one[:, None], axis=0))
    tokens_grad = residual_grad + scale_one[:, None] * gained_one - hidden_in * (scale_one ** 3)[:, None] * lax.optimization_barrier(jnp.mean(gained_one * hidden_in, axis=1))[:, None]
    return (block_out, tokens_grad, attn_gain_grad, query_weight_grad, key_weight_grad, value_weight_grad, query_gain_grad, key_gain_grad, output_weight_grad, ffn_gain_grad, router_weight_grad, gate_experts_grad, up_experts_grad, down_experts_grad)
```

```python
import functools
import math

import jax
import jax.numpy as jnp
from jax import lax
from jax.experimental import pallas as pl
from jax.experimental.pallas import tpu as pltpu
from jax.sharding import PartitionSpec as P

HEAD_DIM = 128
BLK = 64
CAP = 20
EPSILON = 1e-05
ROPE_BASE = 10000.0
AXES = ("ctx", "mp")
F32 = jnp.float32
BF16 = jnp.bfloat16
VMEM_LIMIT = 60 * 1024 * 1024
LANES = 128


def dot_last(a, b):
    return lax.dot_general(a, b, (((1,), (1,)), ((), ())), preferred_element_type=F32)


def dot_first(a, b):
    return lax.dot_general(a, b, (((0,), (0,)), ((), ())), preferred_element_type=F32)


def dot(a, b):
    return jnp.dot(a, b, preferred_element_type=F32)


def rms_scale(values):
    return lax.rsqrt(jnp.mean(values * values, axis=-1, keepdims=True) + EPSILON)


def rope_tables(positions):
    half_dim = HEAD_DIM // 2
    frequency = ROPE_BASE ** (-(jnp.arange(half_dim, dtype=F32) * (2.0 / HEAD_DIM)))
    angles = positions.astype(F32)[:, None] * frequency[None, :]
    cosine_table = jnp.cos(angles)
    sine_table = jnp.sin(angles)
    return (
        jnp.concatenate([cosine_table, cosine_table], 1),
        jnp.concatenate([sine_table, sine_table], 1),
    )


def rotate(values, cosine_table, sine_table):
    half_dim = HEAD_DIM // 2
    turned = jnp.concatenate([-values[:, half_dim:], values[:, :half_dim]], -1)
    return values * cosine_table + turned * sine_table


def unrotate(gradient, cosine_table, sine_table):
    half_dim = HEAD_DIM // 2
    scaled = gradient * sine_table
    turned = jnp.concatenate([scaled[:, half_dim:], -scaled[:, :half_dim]], -1)
    return gradient * cosine_table + turned


def block_positions(block_order, row_ids):
    block_slot = row_ids // BLK
    table_hit = block_slot[:, None] == jnp.arange(block_order.shape[0], dtype=jnp.int32)[None, :]
    first_pos = jnp.sum(jnp.where(table_hit, block_order[None, :], 0), axis=1)
    return first_pos * BLK + row_ids % BLK


def attention_kernel(q_ref, k_ref, v_ref, qpos_ref, kpos_ref, o_ref, lse_ref):
    scores = dot_last(q_ref[...], k_ref[...]) * (1.0 / math.sqrt(HEAD_DIM))
    allowed = kpos_ref[...] <= qpos_ref[...]
    scores = jnp.where(allowed, scores, -1e30)
    row_max = jnp.max(scores, axis=1, keepdims=True)
    weights = jnp.where(allowed, jnp.exp(scores - row_max), 0.0)
    row_total = jnp.sum(weights, axis=1, keepdims=True)
    o_ref[...] = (dot(weights.astype(BF16), v_ref[...]) / row_total).astype(BF16)
    lse_ref[...] = row_max + jnp.log(row_total)


def attention(q, k, v, qpos, kpos):
    rows, keys = q.shape[0], k.shape[0]
    tile = 128
    whole = lambda shape: pl.BlockSpec(shape, lambda i: (0, 0))
    part = lambda width: pl.BlockSpec((tile, width), lambda i: (i, 0))
    return pl.pallas_call(
        attention_kernel,
        grid=(rows // tile,),
        in_specs=[
            part(HEAD_DIM),
            whole((keys, HEAD_DIM)),
            whole((keys, HEAD_DIM)),
            part(1),
            whole((1, keys)),
        ],
        out_specs=[part(HEAD_DIM), part(1)],
        out_shape=[
            jax.ShapeDtypeStruct((rows, HEAD_DIM), BF16),
            jax.ShapeDtypeStruct((rows, 1), F32),
        ],
        compiler_params=pltpu.CompilerParams(vmem_limit_bytes=VMEM_LIMIT),
        name="attention",
    )(q, k, v, qpos, kpos)


def attention_back_kernel(
    q_ref, k_ref, v_ref, g_ref, o_ref, lse_ref, qpos_ref, kpos_ref, dq_ref, dk_ref, dv_ref
):
    scale = 1.0 / math.sqrt(HEAD_DIM)

    @pl.when(pl.program_id(0) == 0)
    def _():
        dk_ref[...] = jnp.zeros_like(dk_ref)
        dv_ref[...] = jnp.zeros_like(dv_ref)

    q, k, g = q_ref[...], k_ref[...], g_ref[...]
    delta = jnp.sum(g.astype(F32) * o_ref[...].astype(F32), axis=1, keepdims=True)
    scores = dot_last(q, k) * scale
    allowed = kpos_ref[...] <= qpos_ref[...]
    weights = jnp.where(allowed, jnp.exp(jnp.where(allowed, scores, 0.0) - lse_ref[...]), 0.0)
    weight_grad = dot_last(g, v_ref[...])
    score_grad = (weights * (weight_grad - delta) * scale).astype(BF16)
    dq_ref[...] = dot(score_grad, k)
    dk_ref[...] += dot_first(score_grad, q)
    dv_ref[...] += dot_first(weights.astype(BF16), g)


def attention_back(q, k, v, g, o, lse, qpos, kpos):
    rows, keys = q.shape[0], k.shape[0]
    tile = 128
    whole = lambda shape: pl.BlockSpec(shape, lambda i: (0, 0))
    part = lambda width: pl.BlockSpec((tile, width), lambda i: (i, 0))
    return pl.pallas_call(
        attention_back_kernel,
        grid=(rows // tile,),
        in_specs=[
            part(HEAD_DIM),
            whole((keys, HEAD_DIM)),
            whole((keys, HEAD_DIM)),
            part(HEAD_DIM),
            part(HEAD_DIM),
            part(1),
            part(1),
            whole((1, keys)),
        ],
        out_specs=[part(HEAD_DIM), whole((keys, HEAD_DIM)), whole((keys, HEAD_DIM))],
        out_shape=[
            jax.ShapeDtypeStruct((rows, HEAD_DIM), F32),
            jax.ShapeDtypeStruct((keys, HEAD_DIM), F32),
            jax.ShapeDtypeStruct((keys, HEAD_DIM), F32),
        ],
        compiler_params=pltpu.CompilerParams(vmem_limit_bytes=VMEM_LIMIT),
        name="attention_back",
    )(q, k, v, g, o, lse, qpos, kpos)


def expert_rows(ref, groups, slots, expert):
    at = pl.multiple_of(expert * slots, 16)
    return jnp.concatenate([ref[g, pl.ds(at, slots), :] for g in range(groups)], axis=0)


def put_rows(ref, groups, slots, expert, values, lo, hi):
    at = pl.multiple_of(expert * slots, 16)
    for g in range(groups):
        ref[g, pl.ds(at, slots), lo:hi] = values[g * slots : (g + 1) * slots]


def grads_in_kernel(groups, slots, parts, *refs):
    pick_ref, down_ref = refs[0], refs[1]
    pieces = refs[2 : 2 + groups * parts]
    rows_out, u_out, rows = refs[2 + groups * parts :]
    step = pl.program_id(0)
    for g in range(groups):

        @pl.when(step == g)
        def _(g=g):
            mine = jnp.concatenate([p[...] for p in pieces[g * parts : (g + 1) * parts]], axis=0)
            rows[g] = dot(pick_ref[g], mine).astype(BF16)

    @pl.when(step >= groups)
    def _():
        mine = expert_rows(rows, groups, slots, step - groups)
        rows_out[0] = mine
        u_out[0] = dot_last(mine, down_ref[0])


def grads_in(pick, pieces, down, slots):
    groups, picked, _ = pick.shape
    experts, hidden, width = down.shape
    parts = len(pieces) // groups
    total = groups * slots
    at = lambda i: jnp.maximum(i - groups, 0)
    return pl.pallas_call(
        functools.partial(grads_in_kernel, groups, slots, parts),
        grid=(groups + experts,),
        in_specs=[
            pl.BlockSpec(pick.shape, lambda i: (0, 0, 0), pipeline_mode=pl.Buffered(1)),
            pl.BlockSpec((1, hidden, width), lambda i: (at(i), 0, 0)),
        ]
        + [
            pl.BlockSpec(p.shape, lambda i: (0, 0), pipeline_mode=pl.Buffered(1)) for p in pieces
        ],
        out_specs=[
            pl.BlockSpec((1, total, width), lambda i: (at(i), 0, 0)),
            pl.BlockSpec((1, total, hidden), lambda i: (at(i), 0, 0)),
        ],
        out_shape=[
            jax.ShapeDtypeStruct((experts, total, width), BF16),
            jax.ShapeDtypeStruct((experts, total, hidden), F32),
        ],
        scratch_shapes=[pltpu.VMEM((groups, picked, width), BF16)],
        compiler_params=pltpu.CompilerParams(vmem_limit_bytes=VMEM_LIMIT),
        name="grads_in",
    )(pick, down, *pieces)


def experts_kernel(groups, slots, parts, experts, expert_count, *refs):
    pick_ref, spread_ref, lane_ref, router_ref, u_ref, gate_ref, up_ref = refs[:7]
    pieces = refs[7 : 7 + groups * parts]
    (
        even_out,
        odd_out,
        rows_out,
        gated_out,
        gate_pre_out,
        up_pre_out,
        rows,
        gate_slots,
        back_rows,
    ) = refs[7 + groups * parts :]
    step = pl.program_id(0)
    width = rows.shape[-1]
    for g in range(groups):

        @pl.when(step == g)
        def _(g=g):
            mine = jnp.concatenate([p[...] for p in pieces[g * parts : (g + 1) * parts]], axis=0)
            rows[g] = dot(pick_ref[g], mine).astype(BF16)
            logits = dot(mine, router_ref[...])
            live = lax.broadcasted_iota(jnp.int32, logits.shape, 1) < expert_count
            logits = jnp.where(live, logits, -1e30)
            top = jnp.max(logits, axis=1, keepdims=True)
            shares = jnp.where(live, jnp.exp(logits - top), 0.0)
            probs = shares / jnp.sum(shares, axis=1, keepdims=True)
            high = probs.astype(BF16)
            low = (probs - high.astype(F32)).astype(BF16)
            picked = dot(pick_ref[g], high) + dot(pick_ref[g], low)
            gate_slots[g] = jnp.sum(picked * lane_ref[...], axis=1, keepdims=True)

    @pl.when((step >= groups) & (step < groups + experts))
    def _():
        e = step - groups
        mine = expert_rows(rows, groups, slots, e)
        gates = expert_rows(gate_slots, groups, slots, e)
        rows_out[0] = mine
        act_gate = dot(mine, gate_ref[0])
        act_up = dot(mine, up_ref[0])
        sigmoid_gate = 1.0 / (1.0 + jnp.exp(-act_gate))
        swish_gate = act_gate * sigmoid_gate
        inner_act = (swish_gate * act_up).astype(BF16).astype(F32)
        raw_grad = u_ref[0]
        gated_out[0] = (inner_act * gates).astype(BF16)
        inner_grad = raw_grad * gates
        gate_pre = (
            inner_grad * act_up * sigmoid_gate * (1.0 + act_gate * (1.0 - sigmoid_gate))
        ).astype(BF16)
        up_pre = (inner_grad * swish_gate).astype(BF16)
        gate_pre_out[0] = gate_pre
        up_pre_out[0] = up_pre
        back = dot_last(gate_pre, gate_ref[0]) + dot_last(up_pre, up_ref[0])
        put_rows(back_rows, groups, slots, e, back.astype(BF16), 0, width)
        dots = jnp.sum(inner_act * raw_grad, axis=1, keepdims=True)
        lanes = lane_ref[pl.ds(pl.multiple_of(e * slots, 16), slots), :]
        spread = dots * jnp.concatenate([lanes] * groups, axis=0)
        put_rows(back_rows, groups, slots, e, spread.astype(BF16), width, width + LANES)

    @pl.when(step >= groups + experts)
    def _():
        g = step - groups - experts
        total = dot(spread_ref[0], back_rows[g]).astype(BF16)
        quarter = total.shape[0] // 4
        even_out[0, 0] = total[:quarter]
        odd_out[0, 0] = total[quarter : 2 * quarter]
        even_out[0, 1] = total[2 * quarter : 3 * quarter]
        odd_out[0, 1] = total[3 * quarter :]


def experts_pass(pick, spread, lanes, router, u, gate, up, pieces, slots, expert_count):
    groups, picked, group_rows = pick.shape
    experts, width, hidden = gate.shape
    parts = len(pieces) // groups
    total = groups * slots
    at = lambda i: jnp.clip(i - groups, 0, experts - 1)
    last = lambda i: jnp.maximum(i - groups - experts, 0)
    fixed = lambda a: pl.BlockSpec(a.shape, lambda i: (0,) * a.ndim, pipeline_mode=pl.Buffered(1))
    by_expert = lambda a, b: pl.BlockSpec((1, a, b), lambda i: (at(i), 0, 0))
    wide = width + LANES
    half = (1, 2, group_rows // 4, wide)
    return pl.pallas_call(
        functools.partial(experts_kernel, groups, slots, parts, experts, expert_count),
        grid=(2 * groups + experts,),
        in_specs=[
            fixed(pick),
            pl.BlockSpec((1, group_rows, picked), lambda i: (last(i), 0, 0)),
            fixed(lanes),
            fixed(router),
            by_expert(total, hidden),
            by_expert(width, hidden),
            by_expert(width, hidden),
        ]
        + [fixed(p) for p in pieces],
        out_specs=[
            pl.BlockSpec(half, lambda i: (last(i), 0, 0, 0)),
            pl.BlockSpec(half, lambda i: (last(i), 0, 0, 0)),
            by_expert(total, width),
            by_expert(total, hidden),
            by_expert(total, hidden),
            by_expert(total, hidden),
        ],
        out_shape=[
            jax.ShapeDtypeStruct((groups,) + half[1:], BF16),
            jax.ShapeDtypeStruct((groups,) + half[1:], BF16),
            jax.ShapeDtypeStruct((experts, total, width), BF16),
            jax.ShapeDtypeStruct((experts, total, hidden), BF16),
            jax.ShapeDtypeStruct((experts, total, hidden), BF16),
            jax.ShapeDtypeStruct((experts, total, hidden), BF16),
        ],
        scratch_shapes=[
            pltpu.VMEM((groups, picked, width), BF16),
            pltpu.VMEM((groups, picked, 1), F32),
            pltpu.VMEM((groups, picked, wide), BF16),
        ],
        compiler_params=pltpu.CompilerParams(vmem_limit_bytes=VMEM_LIMIT),
        name="experts_pass",
    )(pick, spread, lanes, router, u, gate, up, *pieces)


def mix_kernel(groups, slots, experts, spread_ref, gated_ref, down_ref, even_out, odd_out, rows):
    step = pl.program_id(0)

    @pl.when(step < experts)
    def _():
        out = dot(gated_ref[0], down_ref[0]).astype(BF16)
        put_rows(rows, groups, slots, step, out, 0, out.shape[1])

    @pl.when(step >= experts)
    def _():
        total = dot(spread_ref[0], rows[step - experts]).astype(BF16)
        quarter = total.shape[0] // 4
        even_out[0, 0] = total[:quarter]
        odd_out[0, 0] = total[quarter : 2 * quarter]
        even_out[0, 1] = total[2 * quarter : 3 * quarter]
        odd_out[0, 1] = total[3 * quarter :]


def mix(spread, gated, down, slots):
    groups, group_rows, picked = spread.shape
    experts, hidden, width = down.shape
    total = groups * slots
    at = lambda i: jnp.minimum(i, experts - 1)
    last = lambda i: jnp.maximum(i - experts, 0)
    half = (1, 2, group_rows // 4, width)
    return pl.pallas_call(
        functools.partial(mix_kernel, groups, slots, experts),
        grid=(experts + groups,),
        in_specs=[
            pl.BlockSpec((1, group_rows, picked), lambda i: (last(i), 0, 0)),
            pl.BlockSpec((1, total, hidden), lambda i: (at(i), 0, 0)),
            pl.BlockSpec((1, hidden, width), lambda i: (at(i), 0, 0)),
        ],
        out_specs=[pl.BlockSpec(half, lambda i: (last(i), 0, 0, 0))] * 2,
        out_shape=[jax.ShapeDtypeStruct((groups,) + half[1:], BF16)] * 2,
        scratch_shapes=[pltpu.VMEM((groups, picked, width), BF16)],
        compiler_params=pltpu.CompilerParams(vmem_limit_bytes=VMEM_LIMIT),
        name="mix",
    )(spread, gated, down)


def expert_grads_kernel(
    rows_ref, grads_ref, gated_ref, gate_pre_ref, up_pre_ref, gate_out, up_out, down_out
):
    rows = rows_ref[0]
    gate_out[0] = dot_first(rows, gate_pre_ref[0])
    up_out[0] = dot_first(rows, up_pre_ref[0])
    down_out[0] = dot_first(gated_ref[0], grads_ref[0])


def expert_grads(rows, grads, gated, gate_pre, up_pre):
    experts, total, width = rows.shape
    hidden = gated.shape[2]
    spec = lambda a, b: pl.BlockSpec((1, a, b), lambda i: (i, 0, 0))
    return pl.pallas_call(
        expert_grads_kernel,
        grid=(experts,),
        in_specs=[
            spec(total, width),
            spec(total, width),
            spec(total, hidden),
            spec(total, hidden),
            spec(total, hidden),
        ],
        out_specs=[spec(width, hidden), spec(width, hidden), spec(hidden, width)],
        out_shape=[
            jax.ShapeDtypeStruct((experts, width, hidden), F32),
            jax.ShapeDtypeStruct((experts, width, hidden), F32),
            jax.ShapeDtypeStruct((experts, hidden, width), F32),
        ],
        compiler_params=pltpu.CompilerParams(vmem_limit_bytes=VMEM_LIMIT),
        name="expert_grads",
    )(rows, grads, gated, gate_pre, up_pre)


def local(
    tokens,
    out_grad,
    attn_gain,
    query_weight,
    key_weight,
    value_weight,
    query_gain,
    key_gain,
    output_weight,
    ffn_gain,
    router_weight,
    gate_experts,
    up_experts,
    down_experts,
    expert_ids,
    block_order,
):
    ctx_count, mp_count = lax.axis_size("ctx"), lax.axis_size("mp")
    rows_ctx, width = tokens.shape
    heads = query_weight.shape[1] // HEAD_DIM
    seqs = ctx_count // heads
    rows = rows_ctx // mp_count
    piece = heads * rows
    group = mp_count * piece
    experts = gate_experts.shape[0]
    expert_count = experts * ctx_count
    slots = heads * CAP
    weight_rows = query_weight.shape[0]
    top_count = expert_ids.shape[1]

    ctx_id, mp_id = lax.axis_index("ctx"), lax.axis_index("mp")
    head_id, seq_id = ctx_id // seqs, ctx_id % seqs

    def send(x, dh=0, ds=0, dm=0):
        pairs = []
        for c in range(ctx_count):
            for m in range(mp_count):
                h, s = c // seqs, c % seqs
                pairs.append((c * mp_count + m, ((h ^ dh) * seqs + (s ^ ds)) * mp_count + (m ^ dm)))
        return lax.ppermute(x, AXES, pairs)

    def pick_at(stack, index):
        return lax.dynamic_index_in_dim(stack, index, 0, keepdims=False)

    def gather(own, parts):
        line = jnp.concatenate([own] + [send(own, dh=j) for j in range(1, heads)], axis=0)
        pieces = {}
        for js in range(parts):
            for jy in range(mp_count // 2):
                pieces[js, 2 * jy] = line if js == jy == 0 else send(line, ds=js, dm=2 * jy)
        for js in range(parts):
            for jy in range(mp_count // 2):
                pieces[js, 2 * jy + 1] = send(pieces[js, 2 * jy], dm=1)
        return [pieces[js, jm] for js in range(parts) for jm in range(mp_count)]

    def reduce(even, odd, parts):
        other = send(odd, dm=1)
        kept = {
            (js, jy): even[js, jy].astype(F32) + other[js, jy].astype(F32)
            for js in range(parts)
            for jy in range(mp_count // 2)
        }
        total = kept[0, 0]
        for (js, jy), value in kept.items():
            if (js, jy) != (0, 0):
                total = total + send(value.astype(BF16), ds=js, dm=2 * jy).astype(F32)
        total = total.reshape(heads, rows, -1)
        low = total.astype(BF16)
        mine = total[0]
        for j in range(1, heads):
            mine = mine + send(low[j], dh=j).astype(F32)
        return mine

    def over_seqs(own):
        return jnp.stack([own] + [send(own, ds=j) for j in range(1, seqs)], axis=0)

    def over_ctx(own):
        return over_seqs(jnp.stack([own] + [send(own, dh=j) for j in range(1, heads)], axis=0))

    def ctx_order(stack, axis):
        return jnp.concatenate(
            [
                pick_at(pick_at(stack, seq_id ^ s), head_id ^ h)
                for h in range(heads)
                for s in range(seqs)
            ],
            axis=axis,
        )

    def mp_order(parts):
        stack = jnp.stack(parts, axis=0)
        return jnp.concatenate([pick_at(stack, mp_id ^ m) for m in range(mp_count)], axis=0)

    def own_rows(array):
        return lax.dynamic_slice_in_dim(array, mp_id * rows, rows, axis=0)

    row_in = jnp.arange(rows, dtype=jnp.int32)
    mp_of = mp_id ^ jnp.arange(mp_count, dtype=jnp.int32)
    head_of = head_id ^ jnp.arange(heads, dtype=jnp.int32)

    def row_ids(seq):
        return (
            ((head_of[None, :] * seqs + seq) * rows_ctx)[:, :, None]
            + (mp_of * rows)[:, None, None]
            + row_in[None, None, :]
        ).reshape(group)

    tokens_own = own_rows(tokens)
    gains = over_ctx(jnp.stack([attn_gain, ffn_gain], axis=0))
    gain_one, gain_two = [g[None, :].astype(F32) for g in ctx_order(gains, 1)]
    tokens_group = jnp.concatenate(gather(tokens_own, 1), axis=0)

    def head_block(head):
        return jnp.concatenate(
            [
                lax.dynamic_slice_in_dim(w, head * HEAD_DIM, HEAD_DIM, axis=1)
                for w in (query_weight, key_weight, value_weight)
            ],
            axis=1,
        )

    line = jnp.stack(
        [head_block(head_id)] + [send(head_block(head_id ^ j), dh=j) for j in range(1, heads)], 0
    )
    weights_head = ctx_order(over_seqs(line), 0)

    head_gains = over_seqs(jnp.stack([query_gain, key_gain], axis=0))
    head_gains = jnp.concatenate([pick_at(head_gains, seq_id ^ s) for s in range(seqs)], axis=1)
    gain_query, gain_key = [g[None, :].astype(F32) for g in head_gains]

    def out_block(head):
        return lax.dynamic_slice_in_dim(output_weight, head * HEAD_DIM, HEAD_DIM, axis=0)

    line = jnp.stack(
        [out_block(head_id)] + [send(out_block(head_id ^ j), dh=j) for j in range(1, heads)], 0
    )
    output_head = ctx_order(over_seqs(line), 1)
    router_full = ctx_order(over_ctx(router_weight), 0)
    router_wide = jnp.pad(router_full, ((0, 0), (0, LANES - expert_count)))
    ids_all = jnp.stack(gather(own_rows(expert_ids), seqs), 0).reshape(seqs, group, top_count)
    grad_pieces = gather(own_rows(out_grad), seqs)

    mine = ctx_id * experts + jnp.arange(experts, dtype=jnp.int32)
    hit = jnp.any(ids_all[:, :, :, None] == mine, axis=2)
    earlier = jnp.tril(jnp.ones((group, group), BF16), -1)
    slot = jnp.einsum("ij,gje->gie", earlier, hit.astype(BF16), preferred_element_type=F32)
    column = jnp.where(hit, slot.astype(jnp.int32) + jnp.arange(experts) * slots, -1)
    column_row = jnp.swapaxes(column, 1, 2)
    columns = jnp.arange(experts * slots, dtype=jnp.int32)
    chosen = jnp.full((seqs, group, experts * slots), -1, jnp.int32)
    chosen_row = jnp.full((seqs, experts * slots, group), -1, jnp.int32)
    for e in range(experts):
        of_e = columns // slots == e
        chosen = jnp.where(of_e[None, None, :], column[:, :, e : e + 1], chosen)
        chosen_row = jnp.where(of_e[None, :, None], column_row[:, e : e + 1, :], chosen_row)
    spread = (chosen == columns[None, None, :]).astype(BF16)
    pick = (chosen_row == columns[None, :, None]).astype(BF16)
    lane_mask = (
        (ctx_id * experts + columns // slots)[:, None] == jnp.arange(LANES, dtype=jnp.int32)
    ).astype(F32)

    query_pos = block_positions(block_order, row_ids(seq_id))
    key_pos = jnp.concatenate(
        [block_positions(block_order, row_ids(seq_id ^ j)) for j in range(seqs)], axis=0
    )
    cosine_table, sine_table = rope_tables(query_pos)
    hidden = tokens_group.astype(F32)
    scale_one = rms_scale(hidden)
    normed_one = (hidden * scale_one * gain_one).astype(BF16)
    raw = dot(normed_one, weights_head)
    query_raw, key_raw = raw[:, :HEAD_DIM], raw[:, HEAD_DIM : 2 * HEAD_DIM]
    value_own = raw[:, 2 * HEAD_DIM :].astype(BF16)

    def sum_heads(first, second):
        part = jnp.stack([first, second], 0).reshape(2, mp_count // 2, 2, heads, rows)
        part = part + jnp.flip(send(part, dm=1), 2)
        total = part
        for dy in range(mp_count // 2):
            for dh in range(heads):
                if (dy, dh) != (0, 0):
                    other = send(part, dm=2 * dy, dh=dh)
                    if dy:
                        other = jnp.flip(other, 1)
                    order = [j ^ dh for j in range(heads)]
                    total = total + jnp.stack([other[:, :, :, j] for j in order], 3)
        total = total.reshape(2, group)
        return total[0][:, None], total[1][:, None]

    query_sum, key_sum = sum_heads(
        jnp.sum(query_raw * query_raw, axis=1), jnp.sum(key_raw * key_raw, axis=1)
    )
    query_scale = lax.rsqrt(query_sum / width + EPSILON)
    key_scale = lax.rsqrt(key_sum / width + EPSILON)
    query_rot = rotate(query_raw * query_scale * gain_query, cosine_table, sine_table).astype(BF16)
    key_own = rotate(key_raw * key_scale * gain_key, cosine_table, sine_table).astype(BF16)
    key_all = over_seqs(key_own).reshape(seqs * group, HEAD_DIM)
    value_all = over_seqs(value_own).reshape(seqs * group, HEAD_DIM)
    heads_out, log_total = attention(
        query_rot, key_all, value_all, query_pos[:, None], key_pos[None, :]
    )

    def reduce_part(product):
        product = product.reshape(mp_count // 2, 2, piece, width)
        return reduce(product[None, :, 0], product[None, :, 1], 1)

    attended = reduce_part(dot(heads_out, output_head).astype(BF16))
    tokens_mine = tokens_own.astype(F32)
    residual = tokens_mine + attended
    scale_two = rms_scale(residual)
    normed_two = (residual * scale_two * gain_two).astype(BF16)
    router_probs = jax.nn.softmax(dot(normed_two, router_full), axis=-1)

    grad_rows, raw_grads = grads_in(pick, grad_pieces, down_experts, slots)
    normed_pieces = gather(normed_two, seqs)
    even, odd, expert_in, gated, gate_pre, up_pre = experts_pass(
        pick,
        spread,
        lane_mask,
        router_wide,
        raw_grads,
        gate_experts,
        up_experts,
        normed_pieces,
        slots,
        expert_count,
    )
    returned = reduce(even, odd, seqs)
    even, odd = mix(spread, gated, down_experts, slots)
    moe = reduce(even, odd, seqs)
    gate_grad, up_grad, down_grad = expert_grads(expert_in, grad_rows, gated, gate_pre, up_pre)

    def over_mp(own):
        pair = [own, send(own, dm=1)]
        both = send(jnp.concatenate(pair, 0), dm=2)
        return mp_order(pair + [both[:rows], both[rows:]])

    block_out = over_mp((residual + moe).astype(BF16))
    back = returned[:, :width]
    spread_dots = returned[:, width : width + expert_count]
    logit_grad = (
        router_probs * (spread_dots - jnp.sum(router_probs * spread_dots, axis=1, keepdims=True))
    ).astype(BF16)
    logit_all = jnp.concatenate(gather(logit_grad, seqs), axis=0)
    columns_here = jnp.concatenate(
        [
            lax.dynamic_slice_in_dim(p, ctx_id * weight_rows, weight_rows, axis=1)
            for p in normed_pieces
        ],
        axis=0,
    )
    router_grad = dot_first(columns_here, logit_all)
    normed_two_grad = back + dot_last(logit_grad, router_full)
    gained_two = normed_two_grad * gain_two
    ffn_part = jnp.sum(normed_two_grad * residual * scale_two, axis=0)
    residual_grad = (
        own_rows(out_grad).astype(F32)
        + scale_two * gained_two
        - residual * scale_two**3 * jnp.mean(gained_two * residual, axis=1, keepdims=True)
    )

    residual_low = jnp.concatenate(gather(residual_grad.astype(BF16), 1), axis=0)
    heads_grad = dot_last(residual_low, output_head).astype(BF16)
    output_grad = dot_first(residual_low, heads_out)
    query_acc, key_part, value_part = attention_back(
        query_rot,
        key_all,
        value_all,
        heads_grad,
        heads_out,
        log_total,
        query_pos[:, None],
        key_pos[None, :],
    )

    def home(part):
        part = part.reshape(seqs, group, HEAD_DIM)
        total = part[0]
        for j in range(1, seqs):
            total = total + send(part[j].astype(BF16), ds=j).astype(F32)
        return total

    key_acc, value_acc = home(key_part), home(value_part)
    query_normed_grad = unrotate(query_acc, cosine_table, sine_table)
    key_normed_grad = unrotate(key_acc, cosine_table, sine_table)
    value_low = value_acc.astype(BF16)
    query_weighted = query_normed_grad * gain_query
    key_weighted = key_normed_grad * gain_key
    query_dot, key_dot = sum_heads(
        jnp.sum(query_weighted * query_raw, axis=1), jnp.sum(key_weighted * key_raw, axis=1)
    )
    query_coef = query_dot * query_scale**3 / width
    key_coef = key_dot * key_scale**3 / width
    raw_grad = jnp.concatenate(
        [
            (query_weighted * query_scale - query_raw * query_coef).astype(BF16),
            (key_weighted * key_scale - key_raw * key_coef).astype(BF16),
            value_low,
        ],
        axis=1,
    )
    normed_part = dot_last(raw_grad, weights_head)
    attn_part = jnp.sum(normed_part * hidden * scale_one, axis=0)
    weights_grad = dot_first(normed_one, raw_grad)
    normed_one_grad = reduce_part(normed_part.astype(BF16))
    scale_mine = rms_scale(tokens_mine)
    gained_one = normed_one_grad * gain_one
    tokens_grad_own = (
        residual_grad
        + scale_mine * gained_one
        - tokens_mine * scale_mine**3 * jnp.mean(gained_one * tokens_mine, axis=1, keepdims=True)
    )
    tokens_grad = over_mp(tokens_grad_own.astype(BF16)).astype(F32)

    def to_owner(grad):
        grad = grad.astype(BF16).reshape(heads, seqs, weight_rows, -1)
        pick_seq = lambda s: lax.dynamic_index_in_dim(grad, s, 1, keepdims=False)
        total = pick_seq(seq_id).astype(F32)
        for j in range(1, seqs):
            total = total + send(pick_seq(seq_id ^ j), ds=j).astype(F32)
        low = total.astype(BF16)
        blocks = jnp.stack(
            [pick_at(low, head_id)]
            + [send(pick_at(low, head_id ^ j), dh=j) for j in range(1, heads)],
            0,
        )
        return [pick_at(blocks, head_id ^ h).astype(F32) for h in range(heads)]

    by_head = to_owner(weights_grad)
    query_owned, key_owned, value_owned = [
        jnp.concatenate([b[:, i * HEAD_DIM : (i + 1) * HEAD_DIM] for b in by_head], axis=1)
        for i in range(3)
    ]
    output_owned = jnp.concatenate([b.T for b in to_owner(output_grad)], axis=0)

    vectors = jnp.stack([attn_part, ffn_part], 0)
    for dm in (1, 2):
        vectors = vectors + send(vectors, dm=dm)
    vectors = jnp.moveaxis(vectors.reshape(2, heads, seqs, weight_rows), 0, 2)
    owned = None
    for dh in range(heads):
        for ds in range(seqs):
            block = pick_at(pick_at(vectors, head_id ^ dh), seq_id ^ ds)
            owned = block if owned is None else owned + send(block, dh=dh, ds=ds)
    attn_owned, ffn_owned = owned[0], owned[1]

    gain_parts = jnp.stack(
        [
            jnp.sum(query_normed_grad * query_raw * query_scale, axis=0),
            jnp.sum(key_normed_grad * key_raw * key_scale, axis=0),
        ],
        0,
    ).reshape(2, seqs, HEAD_DIM // seqs)
    gain_owned = None
    for ds in range(seqs):
        block = lax.dynamic_index_in_dim(gain_parts, seq_id ^ ds, 1, keepdims=False)
        gain_owned = block if gain_owned is None else gain_owned + send(block, ds=ds)
    return (
        block_out,
        tokens_grad,
        attn_owned,
        query_owned,
        key_owned,
        value_owned,
        gain_owned[0],
        gain_owned[1],
        output_owned,
        ffn_owned,
        router_grad,
        gate_grad,
        up_grad,
        down_grad,
    )


def solution(mesh):
    placed = (
        P("ctx", None),
        P("ctx", None),
        P("ctx"),
        P("ctx", "mp"),
        P("ctx", "mp"),
        P("ctx", "mp"),
        P(("mp", "ctx")),
        P(("mp", "ctx")),
        P("mp", "ctx"),
        P("ctx"),
        P("ctx", None),
        P("ctx", None, "mp"),
        P("ctx", None, "mp"),
        P("ctx", "mp", None),
        P("ctx", None),
        P(),
    )
    return jax.shard_map(
        local,
        mesh=mesh,
        in_specs=placed,
        out_specs=(
            P("ctx", None),
            P("ctx", None),
            P("ctx"),
            P("ctx", "mp"),
            P("ctx", "mp"),
            P("ctx", "mp"),
            P(("mp", "ctx")),
            P(("mp", "ctx")),
            P("mp", "ctx"),
            P("ctx"),
            P("ctx", None),
            P("ctx", None, "mp"),
            P("ctx", None, "mp"),
            P("ctx", "mp", None),
        ),
        check_vma=False,
    )
```
